32 devices in a mesh: prompt: 8 (over y, x, core), seq: 4 (over z).
Axes of the slice: x: 2, y: 2, z: 4, core: 2. Of those that a mesh axis runs over, the one named last changes fastest.
Arguments:
- queries: bfloat16 [8, 512, 4096], P('prompt', 'seq'), may hold values from -8 to 8
- self_keys: bfloat16 [8, 512, 4096], P('prompt', 'seq'), may hold values from -8 to 8
- self_values: bfloat16 [8, 512, 4096], P('prompt', 'seq'), may hold values from -6 to 6
- cross_queries: bfloat16 [8, 512, 4096], P('prompt', 'seq')
- context: bfloat16 [8, 512, 5120], P('prompt', 'seq')
- key_weight: bfloat16 [5120, 4096], P('prompt', 'seq')
- value_weight: bfloat16 [5120, 4096], P('prompt', 'seq'), may hold values from -0.078125 to 0.078125
- lengths: int32 [8], P('prompt'), may hold values from 64 to 512, as said below
Outputs:
- attended: bfloat16 [8, 512, 4096], P('prompt', 'seq')
The draws below stay inside these ranges and needn't reach their ends.
Inputs may be any that keep to these rules, and one draw needn't show every extreme that they name: `lengths`: each prompt's number of text tokens; some prompt has all 512.
All inputs are finite; a program needn't handle non-finite values.
Results may differ from the reference program's by a relative error of at most 0.007.
Values may be sent and summed in bfloat16 or wider, within the bound.
A program may use at most 128 MiB of HBM per device.

```python
import math
import jax
import jax.numpy as jnp
from jax import lax

D = 5120
HD = 128
HEADS = 32
TXT = 512
PROMPTS = 8
SEQ_LEN = 512
HW = 4096


def self_pair(key):
    query_seed, key_seed = jax.random.split(jax.random.fold_in(key, 7), 2)
    full_shape = (PROMPTS, SEQ_LEN, HEADS * HD)
    query_draw = jnp.clip(jax.random.normal(query_seed, full_shape, jnp.float32), -6.0, 6.0)
    key_draw = jnp.clip(jax.random.normal(key_seed, full_shape, jnp.float32), -6.0, 6.0)
    return (query_draw, key_draw)


def cross_parts(key):
    weight_seed, context_seed, query_seed = jax.random.split(jax.random.fold_in(key, 13), 3)
    weight_draw = jax.random.normal(weight_seed, (D, HEADS * HD), jnp.float32) / math.sqrt(D)
    context_draw = jnp.clip(jax.random.normal(context_seed, (PROMPTS, TXT, D), jnp.float32), -6.0, 6.0)
    query_draw = jnp.clip(jax.random.normal(query_seed, (PROMPTS, SEQ_LEN, HEADS * HD), jnp.float32), -6.0, 6.0)
    return (weight_draw, context_draw, query_draw)


def draw_queries(key, part):
    return self_pair(key)[0].astype(jnp.bfloat16)


def draw_self_keys(key, part):
    return self_pair(key)[1].astype(jnp.bfloat16)


def draw_key_weight(key, part):
    return cross_parts(key)[0].astype(jnp.bfloat16)


def draw_context(key, part):
    return cross_parts(key)[1].astype(jnp.bfloat16)


def draw_cross_queries(key, part):
    return cross_parts(key)[2].astype(jnp.bfloat16)


def draw_lengths(key, part):
    first_seed, second_seed, longest_seed = jax.random.split(jax.random.fold_in(key, 29), 3)
    first_draw = jax.random.randint(first_seed, (PROMPTS,), TXT // 8, TXT + 1)
    second_draw = jax.random.randint(second_seed, (PROMPTS,), TXT // 8, TXT + 1)
    shorter = jnp.minimum(first_draw, second_draw)
    longest = jax.random.randint(longest_seed, (), 0, PROMPTS)
    return jnp.where(jnp.arange(PROMPTS) == longest, TXT, shorter).astype(jnp.int32)


def steps_of(rng, dims, cuts, smallest, high):
    gain, own = 1.0, jax.random.fold_in(rng, 6)
    for axis_at, blocks in cuts:
        draws = jnp.exp(jax.random.uniform(jax.random.fold_in(own, axis_at), (blocks,), jnp.float32, smallest / len(cuts), high / len(cuts)))
        gain = gain * jnp.repeat(draws, dims[axis_at] // blocks).reshape([-1 if axis == axis_at else 1 for axis in range(len(dims))])
    return gain


def gaussian(stream_key, dims, scale, bound, shards=(), kind=jnp.bfloat16):
    values = scale * jax.random.normal(stream_key, dims, jnp.float32)
    if shards:
        values = values * steps_of(stream_key, dims, shards, -0.22, 0.18)
    return jnp.clip(values, -bound, bound).astype(kind)


def setup_inputs(seed: int = 0) -> dict:
    splits = jax.random.split(jax.random.key(seed), 9)
    return {
        "queries": draw_queries(jax.random.fold_in(splits[8], 71), 0),
        "self_keys": draw_self_keys(jax.random.fold_in(splits[8], 71), 0),
        "self_values": gaussian(splits[2], (PROMPTS, SEQ_LEN, HW), 1.0, 6.0, ((0, 8), (1, 4))),
        "cross_queries": draw_cross_queries(jax.random.fold_in(splits[8], 71), 0),
        "context": draw_context(jax.random.fold_in(splits[8], 71), 0),
        "key_weight": draw_key_weight(jax.random.fold_in(splits[8], 71), 0),
        "value_weight": gaussian(splits[6], (D, HW), D ** -0.5, 0.078125, ((0, 8), (1, 4))),
        "lengths": draw_lengths(jax.random.fold_in(splits[8], 71), 0),
    }


def attend_head(query_rows, key_rows, value_rows, usable):
    scaling = 1.0 / math.sqrt(HD)
    scores = jnp.dot(query_rows, key_rows.T, preferred_element_type=jnp.float32) * scaling
    row_max = lax.optimization_barrier(jnp.max(jnp.where(usable[None, :], scores, -jnp.inf), axis=1))
    shifted = jnp.where(usable[None, :], scores, row_max[:, None]) - row_max[:, None]
    weights = jnp.where(usable[None, :], jnp.exp(shifted), jnp.zeros_like(shifted))
    totals = lax.optimization_barrier(jnp.sum(weights, axis=1))
    mixed = jnp.dot(weights.astype(jnp.bfloat16), value_rows, preferred_element_type=jnp.float32)
    return (mixed / totals[:, None]).astype(jnp.bfloat16)

def by_head(matrix):
    return matrix.reshape(matrix.shape[0], HEADS, HD).transpose(1, 0, 2)

def reference(queries, self_keys, self_values, cross_queries, context, key_weight, value_weight, lengths):

    def one_prompt(inputs):
        query_all, key_all, value_all, cross_all, context_rows, length = inputs
        text_keys = jnp.dot(context_rows, key_weight, preferred_element_type=jnp.float32).astype(jnp.bfloat16)
        text_values = jnp.dot(context_rows, value_weight, preferred_element_type=jnp.float32).astype(jnp.bfloat16)
        every_token = jnp.ones((SEQ_LEN,), dtype=bool)
        text_usable = jnp.arange(TXT, dtype=jnp.int32) < length

        def one_head(parts):
            query_head, key_head, value_head, cross_head, text_key_head, text_value_head = parts
            self_part = attend_head(query_head, key_head, value_head, every_token)
            cross_part = attend_head(cross_head, text_key_head, text_value_head, text_usable)
            return (self_part.astype(jnp.float32) + cross_part.astype(jnp.float32)).astype(jnp.bfloat16)
        mixed = lax.map(one_head, (by_head(query_all), by_head(key_all), by_head(value_all), by_head(cross_all), by_head(text_keys), by_head(text_values)))
        return mixed.transpose(1, 0, 2).reshape(SEQ_LEN, HEADS * HD)
    return lax.map(one_prompt, (queries, self_keys, self_values, cross_queries, context, lengths))
```

```python
import functools
import math

import jax
import jax.numpy as jnp
from jax import lax
from jax.experimental import pallas as pl
from jax.experimental.pallas import tpu as pltpu
from jax.sharding import PartitionSpec as P

HD = 128
CORES = 2
Q, K, V, CQ = range(4)
INPUTS = (K, V, Q, CQ)
SCORES = 512 * 512


TEXT_ROWS = 16


def group_heads(heads):
    return math.gcd(heads, 2) if heads > 2 else 1


def text_chunk(rows):
    return math.gcd(rows, TEXT_ROWS)


def kernel(
    seq_size,
    prompt_size,
    length_ref,
    q_hbm,
    k_hbm,
    v_hbm,
    cq_hbm,
    ctx_hbm,
    wk_hbm,
    wv_hbm,
    out_hbm,
    q_buf,
    k_buf,
    v_buf,
    cq_buf,
    ctx_buf,
    wk_buf,
    wv_buf,
    text_keys,
    text_values,
    self_buf,
    out_buf,
    local_sem,
    seq_send,
    seq_recv,
    text_send,
    text_recv,
    chip_send,
    chip_recv,
    pair_send,
    pair_recv,
    out_send,
    out_recv,
):
    seq = lax.axis_index("seq")
    prompt = lax.axis_index("prompt")
    chips = prompt_size // CORES
    chip = prompt // CORES
    core = prompt % CORES
    partner = chip * CORES + (1 - core)
    tokens = q_hbm.shape[0]
    text = ctx_hbm.shape[0]
    width = wk_hbm.shape[1]
    depth = wk_hbm.shape[0]
    heads = width // HD
    part = group_heads(heads) * HD
    groups = width // part
    chunk = text_chunk(text)
    chunks = text // chunk
    scaling = 1.0 / math.sqrt(HD)

    def seq_peer(offset):
        return lax.rem(seq + offset, seq_size)

    def seq_source(offset):
        return lax.rem(seq + seq_size - offset, seq_size)

    def chip_peer(offset):
        return lax.rem(chip + offset, chips) * CORES + core

    def chip_source(offset):
        return lax.rem(chip + chips - offset, chips) * CORES + core

    barrier = pltpu.get_barrier_semaphore()
    for offset in range(1, seq_size):
        pl.semaphore_signal(
            barrier, inc=1, device_id={"seq": seq_peer(offset)}, device_id_type=pl.DeviceIdType.MESH
        )
    for offset in range(1, chips):
        pl.semaphore_signal(
            barrier,
            inc=1,
            device_id={"prompt": chip_peer(offset)},
            device_id_type=pl.DeviceIdType.MESH,
        )
    pl.semaphore_signal(
        barrier, inc=1, device_id={"prompt": partner}, device_id_type=pl.DeviceIdType.MESH
    )
    pl.semaphore_wait(barrier, seq_size - 1 + chips - 1 + 1)

    def token_rows(owner):
        return pl.ds(pl.multiple_of(owner * tokens, tokens), tokens)

    def text_rows(owner):
        return pl.ds(pl.multiple_of(owner * text, text), text)

    def group_columns(group):
        return pl.ds(pl.multiple_of(group * part, part), part)

    def head_columns(owner, group):
        return pl.ds(pl.multiple_of(owner * width + group * part, part), part)

    def weight_rows(owner):
        return pl.ds(pl.multiple_of(owner * depth, depth), depth)

    sources = {Q: q_hbm, K: k_hbm, V: v_hbm, CQ: cq_hbm}
    buffers = {Q: q_buf, K: k_buf, V: v_buf, CQ: cq_buf}

    def seq_copy(which, group, offset):
        return pltpu.make_async_remote_copy(
            src_ref=sources[which].at[:, head_columns(seq_peer(offset), group)],
            dst_ref=buffers[which].at[token_rows(seq), group_columns(group)],
            send_sem=seq_send.at[which, group, offset],
            recv_sem=seq_recv.at[which, group, offset],
            device_id={"seq": seq_peer(offset)},
            device_id_type=pl.DeviceIdType.MESH,
        )

    def text_start_here(way, hop):
        if way == 0:
            return (seq >= hop) & (seq + 1 < seq_size)
        return (seq + hop < seq_size) & (seq >= 1)

    def text_lands_here(way, hop):
        return seq >= hop + 1 if way == 0 else seq + 1 + hop < seq_size

    def text_copy(way, hop, index):
        owner = seq - hop if way == 0 else seq + hop
        peer = seq_peer(1 if way == 0 else seq_size - 1)
        start = pl.multiple_of(index * chunk, chunk)
        rows = pl.ds(pl.multiple_of(owner * text + start, chunk), chunk)
        return pltpu.make_async_remote_copy(
            src_ref=ctx_hbm.at[pl.ds(start, chunk)] if hop == 0 else ctx_buf.at[rows],
            dst_ref=ctx_buf.at[rows],
            send_sem=text_send.at[way, hop, index],
            recv_sem=text_recv.at[way, hop, index],
            device_id={"seq": peer},
            device_id_type=pl.DeviceIdType.MESH,
        )

    def loop(count, step):
        def one(index, carry):
            step(index)
            return carry

        lax.fori_loop(0, count, one, 0)

    def start_text(way, hop, index):
        @pl.when(text_start_here(way, hop))
        def _():
            text_copy(way, hop, index).start()

    def wait_text(way, hop, index):
        @pl.when(text_lands_here(way, hop))
        def _():
            text_copy(way, hop, index).wait_recv()

    def relay_text(hop):
        def step(index):
            for way in range(2):
                if hop:
                    wait_text(way, hop - 1, index)
                if hop < hops:
                    start_text(way, hop, index)

        loop(chunks, step)

    weights = ((wk_hbm, wk_buf), (wv_hbm, wv_buf))

    def chip_copy(which, offset):
        shard, gathered = weights[which]
        return pltpu.make_async_remote_copy(
            src_ref=shard,
            dst_ref=gathered.at[weight_rows(prompt)],
            send_sem=chip_send.at[which, offset],
            recv_sem=chip_recv.at[which, offset],
            device_id={"prompt": chip_peer(offset)},
            device_id_type=pl.DeviceIdType.MESH,
        )

    def pair_copy(which, offset):
        shard, gathered = weights[which]
        rows = weight_rows(chip_source(offset))
        return pltpu.make_async_remote_copy(
            src_ref=shard if offset == 0 else gathered.at[rows],
            dst_ref=gathered.at[rows],
            send_sem=pair_send.at[which, offset],
            recv_sem=pair_recv.at[which, offset],
            device_id={"prompt": partner},
            device_id_type=pl.DeviceIdType.MESH,
        )

    def out_copy(offset, group):
        return pltpu.make_async_remote_copy(
            src_ref=out_buf.at[token_rows(seq_source(offset)), group_columns(group)],
            dst_ref=out_hbm.at[:, head_columns(seq, group)],
            send_sem=out_send.at[group, offset],
            recv_sem=out_recv.at[group, offset],
            device_id={"seq": seq_source(offset)},
            device_id_type=pl.DeviceIdType.MESH,
        )

    offsets = sorted(range(1, seq_size), key=lambda offset: abs(2 * offset - seq_size))
    hops = seq_size - 1

    def relays_left(offset):
        right = text_start_here(0, 2)
        left = text_start_here(1, 2)
        ahead = seq + offset < seq_size
        return (ahead & right) | (jnp.logical_not(ahead) & left)

    def start_inputs(late):
        def group_step(group):
            for offset in offsets:

                @pl.when(relays_left(offset) == late)
                def _():
                    for which in INPUTS:
                        seq_copy(which, group, offset).start()

        loop(groups, group_step)

    relay_text(0)
    for which in range(2):
        for offset in range(1, chips):
            chip_copy(which, offset).start()
    for which in range(2):
        pair_copy(which, 0).start()
    own_columns = pl.ds(pl.multiple_of(seq * width, width), width)
    local_copies = [
        pltpu.make_async_copy(
            sources[which].at[:, own_columns], buffers[which].at[token_rows(seq)], local_sem.at[which]
        )
        for which in INPUTS
    ] + [
        pltpu.make_async_copy(ctx_hbm, ctx_buf.at[text_rows(seq)], local_sem.at[4]),
        pltpu.make_async_copy(wk_hbm, wk_buf.at[weight_rows(prompt)], local_sem.at[5]),
        pltpu.make_async_copy(wv_hbm, wv_buf.at[weight_rows(prompt)], local_sem.at[6]),
    ]
    for copy in local_copies:
        copy.start()

    def attend(query, key, value, length):
        scores = lax.dot_general(
            query, key, (((1,), (1,)), ((), ())), preferred_element_type=jnp.float32
        )
        if length is not None:
            slot = lax.broadcasted_iota(jnp.int32, scores.shape, 1)
            scores = jnp.where(slot < length, scores, -jnp.inf)
        row_max = jnp.max(scores, axis=1, keepdims=True)
        exps = jnp.exp((scores - row_max) * scaling)
        totals = jnp.sum(exps, axis=1, keepdims=True)
        mixed = jnp.dot(exps.astype(jnp.bfloat16), value, preferred_element_type=jnp.float32)
        return (mixed / totals).astype(jnp.bfloat16)

    def row_blocks(keys):
        full = tokens * seq_size
        block = full
        while block > tokens and (block * keys > SCORES or full % block):
            block //= 2
        return block, full // block

    def over_rows(keys, step):
        block, count = row_blocks(keys)
        if count == 1:
            step(slice(None))
        else:
            loop(count, lambda index: step(pl.ds(pl.multiple_of(index * block, block), block)))

    def over_heads(group, step):
        def head(index):
            step(pl.ds(pl.multiple_of(group * part + index * HD, HD), HD))

        loop(part // HD, head)

    def self_group(group):
        for which in (K, V, Q):
            for offset in offsets:
                seq_copy(which, group, offset).wait_recv()

        def head(columns):
            key = k_buf[:, columns]
            value = v_buf[:, columns]

            def block(rows):
                self_buf[rows, columns] = attend(q_buf[rows, columns], key, value, None)

            over_rows(k_buf.shape[0], block)

        over_heads(group, head)

    def cross_group(group):
        for offset in offsets:
            seq_copy(CQ, group, offset).wait_recv()
        length = length_ref[0]

        def head(columns):
            key = text_keys[:, columns]
            value = text_values[:, columns]

            def block(rows):
                part = attend(cq_buf[rows, columns], key, value, length)
                out_buf[rows, columns] = (
                    self_buf[rows, columns].astype(jnp.float32) + part.astype(jnp.float32)
                ).astype(jnp.bfloat16)

            over_rows(text_keys.shape[0], block)

        over_heads(group, head)
        for offset in offsets:
            out_copy(offset, group).start()

    def forward(which):
        for offset in range(1, chips):
            chip_copy(which, offset).wait_recv()
            pair_copy(which, offset).start()

    def project(which, target):
        for offset in range(chips):
            pair_copy(which, offset).wait_recv()
        gathered = weights[which][1]
        tile = math.gcd(width, 256)

        def column_tile(index):
            columns = pl.ds(pl.multiple_of(index * tile, tile), tile)
            target[:, columns] = jnp.dot(
                ctx_buf[...], gathered[:, columns], preferred_element_type=jnp.float32
            ).astype(jnp.bfloat16)

        loop(width // tile, column_tile)

    relay_text(1)
    for copy in local_copies:
        copy.wait()
    start_inputs(False)
    for hop in range(2, hops):
        relay_text(hop)
    start_inputs(True)
    forward(0)
    for hop in range(max(hops, 2), hops + 1):
        relay_text(hop)
    project(0, text_keys)
    early = groups // 2
    loop(early, self_group)
    forward(1)
    project(1, text_values)
    loop(early, cross_group)

    def late_group(index):
        self_group(early + index)
        cross_group(early + index)

    loop(groups - early, late_group)
    own = pltpu.make_async_copy(
        out_buf.at[token_rows(seq)], out_hbm.at[:, own_columns], local_sem.at[7]
    )
    own.start()

    def sent_group(group):
        for which in INPUTS:
            for offset in offsets:
                seq_copy(which, group, offset).wait_send()

    loop(groups, sent_group)

    def sent_text(index):
        for hop in range(hops):
            for way in range(2):

                @pl.when(text_start_here(way, hop))
                def _():
                    text_copy(way, hop, index).wait_send()

    loop(chunks, sent_text)
    for which in range(2):
        for offset in range(1, chips):
            chip_copy(which, offset).wait_send()
        for offset in range(chips):
            pair_copy(which, offset).wait_send()
    own.wait()

    def out_group(group):
        for offset in offsets:
            out_copy(offset, group).wait()

    loop(groups, out_group)


def body(
    seq_size,
    prompt_size,
    queries,
    self_keys,
    self_values,
    cross_queries,
    context,
    key_weight,
    value_weight,
    lengths,
):
    tokens = queries.shape[1]
    full = tokens * seq_size
    width = key_weight.shape[1]
    model = context.shape[2]
    chips = prompt_size // CORES
    text_full = context.shape[1] * seq_size
    groups = width // HD // group_heads(width // HD)
    chunks = context.shape[1] // text_chunk(context.shape[1])
    activations = pltpu.VMEM((full, width), jnp.bfloat16)
    texts = pltpu.VMEM((text_full, width), jnp.bfloat16)
    dma = pltpu.SemaphoreType.DMA
    attended = pl.pallas_call(
        functools.partial(kernel, seq_size, prompt_size),
        out_shape=jax.ShapeDtypeStruct(queries.shape[1:], jnp.bfloat16),
        in_specs=[pl.BlockSpec(memory_space=pltpu.SMEM)]
        + [pl.BlockSpec(memory_space=pl.ANY)] * 7,
        out_specs=pl.BlockSpec(memory_space=pl.ANY),
        scratch_shapes=[activations] * 4
        + [pltpu.VMEM((text_full, model), jnp.bfloat16)]
        + [pltpu.VMEM((model, width), jnp.bfloat16)] * 2
        + [texts] * 2
        + [activations] * 2
        + [
            dma((8,)),
            dma((4, groups, seq_size)),
            dma((4, groups, seq_size)),
            dma((2, seq_size, chunks)),
            dma((2, seq_size, chunks)),
            dma((2, chips)),
            dma((2, chips)),
            dma((2, chips)),
            dma((2, chips)),
            dma((groups, seq_size)),
            dma((groups, seq_size)),
        ],
        compiler_params=pltpu.CompilerParams(
            collective_id=0, has_side_effects=True, vmem_limit_bytes=60 * 1024 * 1024
        ),
    )(
        lengths,
        queries[0],
        self_keys[0],
        self_values[0],
        cross_queries[0],
        context[0],
        key_weight,
        value_weight,
    )
    return attended[None]


def solution(mesh):
    in_specs = (
        P("prompt", "seq", None),
        P("prompt", "seq", None),
        P("prompt", "seq", None),
        P("prompt", "seq", None),
        P("prompt", "seq", None),
        P("prompt", "seq"),
        P("prompt", "seq"),
        P("prompt"),
    )
    out_specs = P("prompt", "seq", None)
    step = functools.partial(body, mesh.shape["seq"], mesh.shape["prompt"])
    return jax.shard_map(step, mesh=mesh, in_specs=in_specs, out_specs=out_specs, check_vma=False)
```

```python
import functools
import math

import jax
import jax.numpy as jnp
from jax import lax
from jax.experimental import pallas as pl
from jax.experimental.pallas import tpu as pltpu
from jax.sharding import PartitionSpec as P

HD = 128
CORES = 2
Q, K, V, CQ = range(4)
INPUTS = (K, V, Q, CQ)
SCORES = 512 * 512


TEXT_ROWS = 16


def group_heads(heads):
    return math.gcd(heads, 2) if heads > 2 else 1


def text_chunk(rows):
    return math.gcd(rows, TEXT_ROWS)


def kernel(
    seq_size,
    prompt_size,
    length_ref,
    q_hbm,
    k_hbm,
    v_hbm,
    cq_hbm,
    ctx_hbm,
    wk_hbm,
    wv_hbm,
    out_hbm,
    q_buf,
    k_buf,
    v_buf,
    cq_buf,
    ctx_buf,
    wk_buf,
    wv_buf,
    text_keys,
    text_values,
    self_buf,
    out_buf,
    local_sem,
    seq_send,
    seq_recv,
    text_send,
    text_recv,
    chip_send,
    chip_recv,
    pair_send,
    pair_recv,
    out_send,
    out_recv,
    seq_sem,
    chip_sem,
):
    seq = lax.axis_index("seq")
    prompt = lax.axis_index("prompt")
    chips = prompt_size // CORES
    chip = prompt // CORES
    core = prompt % CORES
    partner = chip * CORES + (1 - core)
    tokens = q_hbm.shape[0]
    text = ctx_hbm.shape[0]
    width = wk_hbm.shape[1]
    depth = wk_hbm.shape[0]
    heads = width // HD
    part = group_heads(heads) * HD
    groups = width // part
    chunk = text_chunk(text)
    chunks = text // chunk
    scaling = 1.0 / math.sqrt(HD)

    def seq_peer(offset):
        return lax.rem(seq + offset, seq_size)

    def seq_source(offset):
        return lax.rem(seq + seq_size - offset, seq_size)

    folds = [1 << bit for bit in range(chips.bit_length() - 1)] if chips & (chips - 1) == 0 else []

    def chip_peer(offset):
        if not folds:
            return lax.rem(chip + offset, chips) * CORES + core
        peer = chip
        for fold in folds:
            if offset & fold:
                peer = peer + fold * (1 - 2 * ((peer // fold) % 2))
        return peer * CORES + core

    def chip_source(offset):
        return chip_peer(offset if folds else chips - offset)

    def seq_greet(semaphores, reach):
        for way, step in enumerate((reach, -reach)):

            @pl.when((seq + step >= 0) & (seq + step < seq_size))
            def _():
                pl.semaphore_signal(
                    semaphores(way),
                    inc=1,
                    device_id={"seq": seq + step},
                    device_id_type=pl.DeviceIdType.MESH,
                )

    def seq_met(semaphore, way, reach):
        step = -reach if way == 0 else reach

        @pl.when((seq + step >= 0) & (seq + step < seq_size))
        def _():
            pl.semaphore_wait(semaphore, 1)

    def chip_greet(semaphore, offset):
        pl.semaphore_signal(
            semaphore,
            inc=1,
            device_id={"prompt": chip_peer(offset)},
            device_id_type=pl.DeviceIdType.MESH,
        )

    near = folds if folds else list(range(1, chips))
    barrier = pltpu.get_barrier_semaphore()
    seq_greet(lambda way: barrier, 1)
    for offset in near:
        chip_greet(barrier, offset)
    pl.semaphore_signal(
        barrier, inc=1, device_id={"prompt": partner}, device_id_type=pl.DeviceIdType.MESH
    )
    inner = jnp.where(seq == 0, 0, 1) + jnp.where(seq == seq_size - 1, 0, 1)
    pl.semaphore_wait(barrier, inner + len(near) + 1)

    def meet_seq():
        reach, turn = 1, 0
        while reach < seq_size - 1:
            seq_greet(lambda way: seq_sem.at[turn, way], reach)
            for way in range(2):
                seq_met(seq_sem.at[turn, way], way, reach)
            reach, turn = 2 * reach, turn + 1

    def meet_chips():
        for turn in range(len(folds) - 1):
            for index, fold in enumerate(folds):
                chip_greet(chip_sem.at[turn, index], fold)
            for index, fold in enumerate(folds):
                pl.semaphore_wait(chip_sem.at[turn, index], 1)

    def token_rows(owner):
        return pl.ds(pl.multiple_of(owner * tokens, tokens), tokens)

    def text_rows(owner):
        return pl.ds(pl.multiple_of(owner * text, text), text)

    def group_columns(group):
        return pl.ds(pl.multiple_of(group * part, part), part)

    def head_columns(owner, group):
        return pl.ds(pl.multiple_of(owner * width + group * part, part), part)

    def weight_rows(owner):
        return pl.ds(pl.multiple_of(owner * depth, depth), depth)

    sources = {Q: q_hbm, K: k_hbm, V: v_hbm, CQ: cq_hbm}
    buffers = {Q: q_buf, K: k_buf, V: v_buf, CQ: cq_buf}

    def seq_copy(which, group, offset):
        return pltpu.make_async_remote_copy(
            src_ref=sources[which].at[:, head_columns(seq_peer(offset), group)],
            dst_ref=buffers[which].at[token_rows(seq), group_columns(group)],
            send_sem=seq_send.at[which, group, offset],
            recv_sem=seq_recv.at[which, group, offset],
            device_id={"seq": seq_peer(offset)},
            device_id_type=pl.DeviceIdType.MESH,
        )

    def text_start_here(way, hop):
        if way == 0:
            return (seq >= hop) & (seq + 1 < seq_size)
        return (seq + hop < seq_size) & (seq >= 1)

    def text_lands_here(way, hop):
        return seq >= hop + 1 if way == 0 else seq + 1 + hop < seq_size

    def text_copy(way, hop, index):
        owner = seq - hop if way == 0 else seq + hop
        peer = seq_peer(1 if way == 0 else seq_size - 1)
        start = pl.multiple_of(index * chunk, chunk)
        rows = pl.ds(pl.multiple_of(owner * text + start, chunk), chunk)
        return pltpu.make_async_remote_copy(
            src_ref=ctx_hbm.at[pl.ds(start, chunk)] if hop == 0 else ctx_buf.at[rows],
            dst_ref=ctx_buf.at[rows],
            send_sem=text_send.at[way, hop, index],
            recv_sem=text_recv.at[way, hop, index],
            device_id={"seq": peer},
            device_id_type=pl.DeviceIdType.MESH,
        )

    def loop(count, step):
        def one(index, carry):
            step(index)
            return carry

        lax.fori_loop(0, count, one, 0)

    def start_text(way, hop, index):
        @pl.when(text_start_here(way, hop))
        def _():
            text_copy(way, hop, index).start()

    def wait_text(way, hop, index):
        @pl.when(text_lands_here(way, hop))
        def _():
            text_copy(way, hop, index).wait_recv()

    def relay_text(hop):
        def step(index):
            for way in range(2):
                if hop:
                    wait_text(way, hop - 1, index)
                if hop < hops:
                    start_text(way, hop, index)

        loop(chunks, step)

    weights = ((wk_hbm, wk_buf), (wv_hbm, wv_buf))

    def chip_copy(which, offset):
        shard, gathered = weights[which]
        return pltpu.make_async_remote_copy(
            src_ref=shard,
            dst_ref=gathered.at[weight_rows(prompt)],
            send_sem=chip_send.at[which, offset],
            recv_sem=chip_recv.at[which, offset],
            device_id={"prompt": chip_peer(offset)},
            device_id_type=pl.DeviceIdType.MESH,
        )

    def pair_copy(which, offset):
        shard, gathered = weights[which]
        rows = weight_rows(chip_source(offset))
        return pltpu.make_async_remote_copy(
            src_ref=shard if offset == 0 else gathered.at[rows],
            dst_ref=gathered.at[rows],
            send_sem=pair_send.at[which, offset],
            recv_sem=pair_recv.at[which, offset],
            device_id={"prompt": partner},
            device_id_type=pl.DeviceIdType.MESH,
        )

    def out_copy(offset, group):
        return pltpu.make_async_remote_copy(
            src_ref=out_buf.at[token_rows(seq_source(offset)), group_columns(group)],
            dst_ref=out_hbm.at[:, head_columns(seq, group)],
            send_sem=out_send.at[group, offset],
            recv_sem=out_recv.at[group, offset],
            device_id={"seq": seq_source(offset)},
            device_id_type=pl.DeviceIdType.MESH,
        )

    offsets = sorted(range(1, seq_size), key=lambda offset: abs(2 * offset - seq_size))
    hops = seq_size - 1

    def relays_left(offset):
        right = text_start_here(0, 2)
        left = text_start_here(1, 2)
        ahead = seq + offset < seq_size
        return (ahead & right) | (jnp.logical_not(ahead) & left)

    def start_inputs(late):
        def group_step(group):
            for offset in offsets:

                @pl.when(relays_left(offset) == late)
                def _():
                    for which in INPUTS:
                        seq_copy(which, group, offset).start()

        loop(groups, group_step)

    relay_text(0)
    for offset in near:
        chip_copy(0, offset).start()
    meet_seq()
    meet_chips()
    for which in range(2):
        for offset in range(1, chips):
            if which or offset not in near:
                chip_copy(which, offset).start()
    for which in range(2):
        pair_copy(which, 0).start()
    own_columns = pl.ds(pl.multiple_of(seq * width, width), width)
    local_copies = [
        pltpu.make_async_copy(
            sources[which].at[:, own_columns], buffers[which].at[token_rows(seq)], local_sem.at[which]
        )
        for which in INPUTS
    ] + [
        pltpu.make_async_copy(ctx_hbm, ctx_buf.at[text_rows(seq)], local_sem.at[4]),
        pltpu.make_async_copy(wk_hbm, wk_buf.at[weight_rows(prompt)], local_sem.at[5]),
        pltpu.make_async_copy(wv_hbm, wv_buf.at[weight_rows(prompt)], local_sem.at[6]),
    ]
    for copy in local_copies:
        copy.start()

    def attend(query, key, value, length):
        scores = lax.dot_general(
            query, key, (((1,), (1,)), ((), ())), preferred_element_type=jnp.float32
        )
        if length is not None:
            slot = lax.broadcasted_iota(jnp.int32, scores.shape, 1)
            scores = jnp.where(slot < length, scores, -jnp.inf)
        row_max = jnp.max(scores, axis=1, keepdims=True)
        exps = jnp.exp((scores - row_max) * scaling)
        totals = jnp.sum(exps, axis=1, keepdims=True)
        mixed = jnp.dot(exps.astype(jnp.bfloat16), value, preferred_element_type=jnp.float32)
        return (mixed / totals).astype(jnp.bfloat16)

    def row_blocks(keys):
        full = tokens * seq_size
        block = full
        while block > tokens and (block * keys > SCORES or full % block):
            block //= 2
        return block, full // block

    def over_rows(keys, step):
        block, count = row_blocks(keys)
        if count == 1:
            step(slice(None))
        else:
            loop(count, lambda index: step(pl.ds(pl.multiple_of(index * block, block), block)))

    def over_heads(group, step):
        def head(index):
            step(pl.ds(pl.multiple_of(group * part + index * HD, HD), HD))

        loop(part // HD, head)

    def self_group(group):
        for which in (K, V, Q):
            for offset in offsets:
                seq_copy(which, group, offset).wait_recv()

        def head(columns):
            key = k_buf[:, columns]
            value = v_buf[:, columns]

            def block(rows):
                self_buf[rows, columns] = attend(q_buf[rows, columns], key, value, None)

            over_rows(k_buf.shape[0], block)

        over_heads(group, head)

    def cross_group(group):
        for offset in offsets:
            seq_copy(CQ, group, offset).wait_recv()
        length = length_ref[0]

        def head(columns):
            key = text_keys[:, columns]
            value = text_values[:, columns]

            def block(rows):
                part = attend(cq_buf[rows, columns], key, value, length)
                out_buf[rows, columns] = (
                    self_buf[rows, columns].astype(jnp.float32) + part.astype(jnp.float32)
                ).astype(jnp.bfloat16)

            over_rows(text_keys.shape[0], block)

        over_heads(group, head)
        for offset in offsets:
            out_copy(offset, group).start()

    def forward(which):
        for offset in range(1, chips):
            chip_copy(which, offset).wait_recv()
            pair_copy(which, offset).start()

    def project(which, target):
        for offset in range(chips):
            pair_copy(which, offset).wait_recv()
        gathered = weights[which][1]
        tile = math.gcd(width, 256)

        def column_tile(index):
            columns = pl.ds(pl.multiple_of(index * tile, tile), tile)
            target[:, columns] = jnp.dot(
                ctx_buf[...], gathered[:, columns], preferred_element_type=jnp.float32
            ).astype(jnp.bfloat16)

        loop(width // tile, column_tile)

    relay_text(1)
    for copy in local_copies:
        copy.wait()
    start_inputs(False)
    for hop in range(2, hops):
        relay_text(hop)
    start_inputs(True)
    forward(0)
    for hop in range(max(hops, 2), hops + 1):
        relay_text(hop)
    project(0, text_keys)
    early = groups // 2
    loop(early, self_group)
    forward(1)
    project(1, text_values)
    loop(early, cross_group)

    def late_group(index):
        self_group(early + index)
        cross_group(early + index)

    loop(groups - early, late_group)
    own = pltpu.make_async_copy(
        out_buf.at[token_rows(seq)], out_hbm.at[:, own_columns], local_sem.at[7]
    )
    own.start()

    def sent_group(group):
        for which in INPUTS:
            for offset in offsets:
                seq_copy(which, group, offset).wait_send()

    loop(groups, sent_group)

    def sent_text(index):
        for hop in range(hops):
            for way in range(2):

                @pl.when(text_start_here(way, hop))
                def _():
                    text_copy(way, hop, index).wait_send()

    loop(chunks, sent_text)
    for which in range(2):
        for offset in range(1, chips):
            chip_copy(which, offset).wait_send()
        for offset in range(chips):
            pair_copy(which, offset).wait_send()
    own.wait()

    def out_group(group):
        for offset in offsets:
            out_copy(offset, group).wait()

    loop(groups, out_group)


def body(
    seq_size,
    prompt_size,
    queries,
    self_keys,
    self_values,
    cross_queries,
    context,
    key_weight,
    value_weight,
    lengths,
):
    tokens = queries.shape[1]
    full = tokens * seq_size
    width = key_weight.shape[1]
    model = context.shape[2]
    chips = prompt_size // CORES
    text_full = context.shape[1] * seq_size
    groups = width // HD // group_heads(width // HD)
    chunks = context.shape[1] // text_chunk(context.shape[1])
    activations = pltpu.VMEM((full, width), jnp.bfloat16)
    texts = pltpu.VMEM((text_full, width), jnp.bfloat16)
    dma = pltpu.SemaphoreType.DMA
    attended = pl.pallas_call(
        functools.partial(kernel, seq_size, prompt_size),
        out_shape=jax.ShapeDtypeStruct(queries.shape[1:], jnp.bfloat16),
        in_specs=[pl.BlockSpec(memory_space=pltpu.SMEM)]
        + [pl.BlockSpec(memory_space=pltpu.HBM)] * 7,
        out_specs=pl.BlockSpec(memory_space=pl.ANY),
        scratch_shapes=[activations] * 4
        + [pltpu.VMEM((text_full, model), jnp.bfloat16)]
        + [pltpu.VMEM((model, width), jnp.bfloat16)] * 2
        + [texts] * 2
        + [activations] * 2
        + [
            dma((8,)),
            dma((4, groups, seq_size)),
            dma((4, groups, seq_size)),
            dma((2, seq_size, chunks)),
            dma((2, seq_size, chunks)),
            dma((2, chips)),
            dma((2, chips)),
            dma((2, chips)),
            dma((2, chips)),
            dma((groups, seq_size)),
            dma((groups, seq_size)),
            pltpu.SemaphoreType.REGULAR((seq_size.bit_length(), 2)),
            pltpu.SemaphoreType.REGULAR((chips.bit_length(), chips.bit_length())),
        ],
        compiler_params=pltpu.CompilerParams(
            collective_id=0, has_side_effects=True, vmem_limit_bytes=48 * 1024 * 1024
        ),
    )(
        lengths,
        *(
            pltpu.with_memory_space_constraint(operand, pltpu.HBM)
            for operand in (
                queries[0],
                self_keys[0],
                self_values[0],
                cross_queries[0],
                context[0],
                key_weight,
                value_weight,
            )
        ),
    )
    return attended[None]


def solution(mesh):
    in_specs = (
        P("prompt", "seq", None),
        P("prompt", "seq", None),
        P("prompt", "seq", None),
        P("prompt", "seq", None),
        P("prompt", "seq", None),
        P("prompt", "seq"),
        P("prompt", "seq"),
        P("prompt"),
    )
    out_specs = P("prompt", "seq", None)
    step = functools.partial(body, mesh.shape["seq"], mesh.shape["prompt"])
    return jax.shard_map(step, mesh=mesh, in_specs=in_specs, out_specs=out_specs, check_vma=False)
```

```python
import functools
import math

import jax
import jax.numpy as jnp
from jax import lax
from jax.experimental import pallas as pl
from jax.experimental.pallas import tpu as pltpu
from jax.sharding import PartitionSpec as P

HD = 128
CORES = 2
Q, K, V, CQ = range(4)
INPUTS = (K, V, Q, CQ)
SCORES = 512 * 512


TEXT_ROWS = 16


def group_heads(heads):
    return math.gcd(heads, 2) if heads > 2 else 1


def text_chunk(rows):
    return math.gcd(rows, TEXT_ROWS)


def kernel(
    seq_size,
    prompt_size,
    length_ref,
    q_hbm,
    k_hbm,
    v_hbm,
    cq_hbm,
    ctx_hbm,
    wk_hbm,
    wv_hbm,
    out_hbm,
    q_buf,
    k_buf,
    v_buf,
    cq_buf,
    ctx_buf,
    wk_buf,
    wv_buf,
    text_keys,
    text_values,
    self_buf,
    out_buf,
    aid_q,
    aid_k,
    aid_v,
    aid_out,
    local_sem,
    seq_send,
    seq_recv,
    text_send,
    text_recv,
    chip_send,
    chip_recv,
    pair_send,
    pair_recv,
    out_send,
    out_recv,
    seq_sem,
    chip_sem,
    aid_send,
    aid_recv,
    aid_local,
    aid_done,
):
    seq = lax.axis_index("seq")
    prompt = lax.axis_index("prompt")
    chips = prompt_size // CORES
    chip = prompt // CORES
    core = prompt % CORES
    partner = chip * CORES + (1 - core)
    tokens = q_hbm.shape[0]
    text = ctx_hbm.shape[0]
    width = wk_hbm.shape[1]
    depth = wk_hbm.shape[0]
    heads = width // HD
    part = group_heads(heads) * HD
    groups = width // part
    chunk = text_chunk(text)
    chunks = text // chunk
    scaling = 1.0 / math.sqrt(HD)

    def seq_peer(offset):
        return lax.rem(seq + offset, seq_size)

    def seq_source(offset):
        return lax.rem(seq + seq_size - offset, seq_size)

    folds = [1 << bit for bit in range(chips.bit_length() - 1)] if chips & (chips - 1) == 0 else []

    def chip_peer(offset):
        if not folds:
            return lax.rem(chip + offset, chips) * CORES + core
        peer = chip
        for fold in folds:
            if offset & fold:
                peer = peer + fold * (1 - 2 * ((peer // fold) % 2))
        return peer * CORES + core

    def chip_source(offset):
        return chip_peer(offset if folds else chips - offset)

    def seq_greet(semaphores, reach):
        for way, step in enumerate((reach, -reach)):

            @pl.when((seq + step >= 0) & (seq + step < seq_size))
            def _():
                pl.semaphore_signal(
                    semaphores(way),
                    inc=1,
                    device_id={"seq": seq + step},
                    device_id_type=pl.DeviceIdType.MESH,
                )

    def seq_met(semaphore, way, reach):
        step = -reach if way == 0 else reach

        @pl.when((seq + step >= 0) & (seq + step < seq_size))
        def _():
            pl.semaphore_wait(semaphore, 1)

    def chip_greet(semaphore, offset):
        pl.semaphore_signal(
            semaphore,
            inc=1,
            device_id={"prompt": chip_peer(offset)},
            device_id_type=pl.DeviceIdType.MESH,
        )

    near = folds if folds else list(range(1, chips))
    barrier = pltpu.get_barrier_semaphore()
    seq_greet(lambda way: barrier, 1)
    for offset in near:
        chip_greet(barrier, offset)
    pl.semaphore_signal(
        barrier, inc=1, device_id={"prompt": partner}, device_id_type=pl.DeviceIdType.MESH
    )
    inner = jnp.where(seq == 0, 0, 1) + jnp.where(seq == seq_size - 1, 0, 1)
    pl.semaphore_wait(barrier, inner + len(near) + 1)

    def meet_seq():
        reach, turn = 1, 0
        while reach < seq_size - 1:
            seq_greet(lambda way: seq_sem.at[turn, way], reach)
            for way in range(2):
                seq_met(seq_sem.at[turn, way], way, reach)
            reach, turn = 2 * reach, turn + 1

    def meet_chips():
        for turn in range(len(folds) - 1):
            for index, fold in enumerate(folds):
                chip_greet(chip_sem.at[turn, index], fold)
            for index, fold in enumerate(folds):
                pl.semaphore_wait(chip_sem.at[turn, index], 1)

    def token_rows(owner):
        return pl.ds(pl.multiple_of(owner * tokens, tokens), tokens)

    def text_rows(owner):
        return pl.ds(pl.multiple_of(owner * text, text), text)

    def group_columns(group):
        return pl.ds(pl.multiple_of(group * part, part), part)

    def head_columns(owner, group):
        return pl.ds(pl.multiple_of(owner * width + group * part, part), part)

    def weight_rows(owner):
        return pl.ds(pl.multiple_of(owner * depth, depth), depth)

    sources = {Q: q_hbm, K: k_hbm, V: v_hbm, CQ: cq_hbm}
    buffers = {Q: q_buf, K: k_buf, V: v_buf, CQ: cq_buf}

    def seq_copy(which, group, offset):
        return pltpu.make_async_remote_copy(
            src_ref=sources[which].at[:, head_columns(seq_peer(offset), group)],
            dst_ref=buffers[which].at[token_rows(seq), group_columns(group)],
            send_sem=seq_send.at[which, group, offset],
            recv_sem=seq_recv.at[which, group, offset],
            device_id={"seq": seq_peer(offset)},
            device_id_type=pl.DeviceIdType.MESH,
        )

    aided = seq_size >= 4
    at_end = (seq == 0) | (seq == seq_size - 1)
    at_helper = (seq == 1) | (seq == seq_size - 2)
    sides = ((0, 1), (seq_size - 1, seq_size - 2)) if aided else ()
    aids = {Q: aid_q, K: aid_k, V: aid_v}

    def to_end(offset):
        peer = seq_peer(offset)
        return (peer == 0) | (peer == seq_size - 1)

    def aid_copy(which, side, source):
        end, helper = sides[side]
        return pltpu.make_async_remote_copy(
            src_ref=sources[which].at[:, head_columns(end, 0)],
            dst_ref=aids[which].at[token_rows(source)],
            send_sem=aid_send.at[which, side],
            recv_sem=aid_recv.at[which, source],
            device_id={"seq": helper},
            device_id_type=pl.DeviceIdType.MESH,
        )

    def aid_own(which, side):
        return pltpu.make_async_copy(
            sources[which].at[:, head_columns(sides[side][0], 0)],
            aids[which].at[token_rows(seq)],
            aid_local.at[which],
        )

    def aid_result():
        return pltpu.make_async_remote_copy(
            src_ref=aid_out,
            dst_ref=self_buf.at[:, group_columns(0)],
            send_sem=aid_done.at[0],
            recv_sem=aid_done.at[1],
            device_id={"seq": jnp.where(seq == 1, 0, seq_size - 1)},
            device_id_type=pl.DeviceIdType.MESH,
        )

    def start_aid():
        for side, (end, helper) in enumerate(sides):

            @pl.when(seq != helper)
            def _():
                for which in (K, V, Q):
                    aid_copy(which, side, seq).start()

            @pl.when(seq == helper)
            def _():
                for which in (K, V, Q):
                    aid_own(which, side).start()

    def sent_aid():
        for side, (end, helper) in enumerate(sides):

            @pl.when(seq != helper)
            def _():
                for which in (K, V, Q):
                    aid_copy(which, side, seq).wait_send()

        if aided:

            @pl.when(at_helper)
            def _():
                aid_result().wait_send()

    def text_start_here(way, hop):
        if way == 0:
            return (seq >= hop) & (seq + 1 < seq_size)
        return (seq + hop < seq_size) & (seq >= 1)

    def text_lands_here(way, hop):
        return seq >= hop + 1 if way == 0 else seq + 1 + hop < seq_size

    def text_copy(way, hop, index):
        owner = seq - hop if way == 0 else seq + hop
        peer = seq_peer(1 if way == 0 else seq_size - 1)
        start = pl.multiple_of(index * chunk, chunk)
        rows = pl.ds(pl.multiple_of(owner * text + start, chunk), chunk)
        return pltpu.make_async_remote_copy(
            src_ref=ctx_hbm.at[pl.ds(start, chunk)] if hop == 0 else ctx_buf.at[rows],
            dst_ref=ctx_buf.at[rows],
            send_sem=text_send.at[way, hop, index],
            recv_sem=text_recv.at[way, hop, index],
            device_id={"seq": peer},
            device_id_type=pl.DeviceIdType.MESH,
        )

    def loop(count, step):
        def one(index, carry):
            step(index)
            return carry

        lax.fori_loop(0, count, one, 0)

    def start_text(way, hop, index):
        @pl.when(text_start_here(way, hop))
        def _():
            text_copy(way, hop, index).start()

    def wait_text(way, hop, index):
        @pl.when(text_lands_here(way, hop))
        def _():
            text_copy(way, hop, index).wait_recv()

    def relay_text(hop):
        def step(index):
            for way in range(2):
                if hop:
                    wait_text(way, hop - 1, index)
                if hop < hops:
                    start_text(way, hop, index)

        loop(chunks, step)

    weights = ((wk_hbm, wk_buf), (wv_hbm, wv_buf))

    def chip_copy(which, offset):
        shard, gathered = weights[which]
        return pltpu.make_async_remote_copy(
            src_ref=shard,
            dst_ref=gathered.at[weight_rows(prompt)],
            send_sem=chip_send.at[which, offset],
            recv_sem=chip_recv.at[which, offset],
            device_id={"prompt": chip_peer(offset)},
            device_id_type=pl.DeviceIdType.MESH,
        )

    def pair_copy(which, offset):
        shard, gathered = weights[which]
        rows = weight_rows(chip_source(offset))
        return pltpu.make_async_remote_copy(
            src_ref=shard if offset == 0 else gathered.at[rows],
            dst_ref=gathered.at[rows],
            send_sem=pair_send.at[which, offset],
            recv_sem=pair_recv.at[which, offset],
            device_id={"prompt": partner},
            device_id_type=pl.DeviceIdType.MESH,
        )

    def out_copy(offset, group):
        return pltpu.make_async_remote_copy(
            src_ref=out_buf.at[token_rows(seq_source(offset)), group_columns(group)],
            dst_ref=out_hbm.at[:, head_columns(seq, group)],
            send_sem=out_send.at[group, offset],
            recv_sem=out_recv.at[group, offset],
            device_id={"seq": seq_source(offset)},
            device_id_type=pl.DeviceIdType.MESH,
        )

    offsets = sorted(range(1, seq_size), key=lambda offset: abs(2 * offset - seq_size))
    hops = seq_size - 1

    def relays_left(offset):
        right = text_start_here(0, 2)
        left = text_start_here(1, 2)
        ahead = seq + offset < seq_size
        return (ahead & right) | (jnp.logical_not(ahead) & left)

    def start_inputs(late):
        if not late:
            start_aid()

        def start_one(group, offset, valid):
            @pl.when(valid & (relays_left(offset) == late))
            def _():
                @pl.when((group > 0) | jnp.logical_not(aided & to_end(offset)))
                def _():
                    for which in (K, V, Q):
                        seq_copy(which, group, offset).start()

                seq_copy(CQ, group, offset).start()

        batch = max(groups // 1, 1)

        def batch_step(index):
            for distance in range(1, seq_size):

                def group_step(group):
                    start_one(index * batch + group, distance, seq + distance < seq_size)
                    start_one(index * batch + group, seq_size - distance, seq >= distance)

                loop(batch, group_step)

        loop(groups // batch, batch_step)

    relay_text(0)
    for offset in near:
        chip_copy(0, offset).start()
    meet_seq()
    meet_chips()
    for which in range(2):
        for offset in range(1, chips):
            if which or offset not in near:
                chip_copy(which, offset).start()
    for which in range(2):
        pair_copy(which, 0).start()
    own_columns = pl.ds(pl.multiple_of(seq * width, width), width)
    local_copies = [
        pltpu.make_async_copy(
            sources[which].at[:, own_columns], buffers[which].at[token_rows(seq)], local_sem.at[which]
        )
        for which in INPUTS
    ] + [
        pltpu.make_async_copy(ctx_hbm, ctx_buf.at[text_rows(seq)], local_sem.at[4]),
        pltpu.make_async_copy(wk_hbm, wk_buf.at[weight_rows(prompt)], local_sem.at[5]),
        pltpu.make_async_copy(wv_hbm, wv_buf.at[weight_rows(prompt)], local_sem.at[6]),
    ]
    for copy in local_copies:
        copy.start()

    def attend(query, key, value, length):
        scores = lax.dot_general(
            query, key, (((1,), (1,)), ((), ())), preferred_element_type=jnp.float32
        )
        if length is not None:
            slot = lax.broadcasted_iota(jnp.int32, scores.shape, 1)
            scores = jnp.where(slot < length, scores, -jnp.inf)
        row_max = jnp.max(scores, axis=1, keepdims=True)
        exps = jnp.exp((scores - row_max) * scaling)
        totals = jnp.sum(exps, axis=1, keepdims=True)
        mixed = jnp.dot(exps.astype(jnp.bfloat16), value, preferred_element_type=jnp.float32)
        return (mixed / totals).astype(jnp.bfloat16)

    def row_blocks(keys):
        full = tokens * seq_size
        block = full
        while block > tokens and (block * keys > SCORES or full % block):
            block //= 2
        return block, full // block

    def over_rows(keys, step):
        block, count = row_blocks(keys)
        if count == 1:
            step(slice(None))
        else:
            loop(count, lambda index: step(pl.ds(pl.multiple_of(index * block, block), block)))

    def over_heads(group, step):
        def head(index):
            step(pl.ds(pl.multiple_of(group * part + index * HD, HD), HD))

        loop(part // HD, head)

    def self_group(group):
        for which in (K, V, Q):
            for offset in offsets:
                seq_copy(which, group, offset).wait_recv()

        def head(columns):
            key = k_buf[:, columns]
            value = v_buf[:, columns]

            def block(rows):
                self_buf[rows, columns] = attend(q_buf[rows, columns], key, value, None)

            over_rows(k_buf.shape[0], block)

        over_heads(group, head)

    def aid_group():
        @pl.when(at_helper)
        def _():
            for source in range(seq_size):

                @pl.when(seq != source)
                def _():
                    for which in (K, V, Q):
                        aid_copy(which, 0, source).wait_recv()

            for side, (end, helper) in enumerate(sides):

                @pl.when(seq == helper)
                def _():
                    for which in (K, V, Q):
                        aid_own(which, side).wait()

            def head(index):
                columns = pl.ds(pl.multiple_of(index * HD, HD), HD)
                key = aid_k[:, columns]
                value = aid_v[:, columns]

                def block(rows):
                    aid_out[rows, columns] = attend(aid_q[rows, columns], key, value, None)

                over_rows(aid_k.shape[0], block)

            loop(part // HD, head)
            aid_result().start()

    def first_self():
        if not aided:
            self_group(0)
            return
        aid_group()

        @pl.when(jnp.logical_not(at_end))
        def _():
            self_group(0)

    def first_cross():
        if aided:

            @pl.when(at_end)
            def _():
                aid_result().wait_recv()

        cross_group(0)

    def cross_group(group):
        for offset in offsets:
            seq_copy(CQ, group, offset).wait_recv()
        length = length_ref[0]

        def head(columns):
            key = text_keys[:, columns]
            value = text_values[:, columns]

            def block(rows):
                part = attend(cq_buf[rows, columns], key, value, length)
                out_buf[rows, columns] = (
                    self_buf[rows, columns].astype(jnp.float32) + part.astype(jnp.float32)
                ).astype(jnp.bfloat16)

            over_rows(text_keys.shape[0], block)

        over_heads(group, head)
        for offset in offsets:
            out_copy(offset, group).start()

    def forward(which):
        for offset in range(1, chips):
            chip_copy(which, offset).wait_recv()
            pair_copy(which, offset).start()

    def project(which, target):
        for offset in range(chips):
            pair_copy(which, offset).wait_recv()
        gathered = weights[which][1]
        tile = math.gcd(width, 256)

        def column_tile(index):
            columns = pl.ds(pl.multiple_of(index * tile, tile), tile)
            target[:, columns] = jnp.dot(
                ctx_buf[...], gathered[:, columns], preferred_element_type=jnp.float32
            ).astype(jnp.bfloat16)

        loop(width // tile, column_tile)

    relay_text(1)
    for copy in local_copies:
        copy.wait()
    start_inputs(False)
    start_inputs(True)
    for hop in range(2, hops):
        relay_text(hop)
    forward(0)
    for hop in range(max(hops, 2), hops + 1):
        relay_text(hop)
    project(0, text_keys)
    early = max(groups // 2, 1)
    first_self()
    loop(early - 1, lambda index: self_group(1 + index))
    forward(1)
    project(1, text_values)
    loop(early - 1, lambda index: cross_group(1 + index))

    def late_group(group):
        self_group(group)
        cross_group(group)

    loop(groups - early - 1, lambda index: late_group(early + index))
    first_cross()
    if groups > early:
        late_group(groups - 1)
    own = pltpu.make_async_copy(
        out_buf.at[token_rows(seq)], out_hbm.at[:, own_columns], local_sem.at[7]
    )
    own.start()

    def sent_group(group):
        for offset in offsets:

            @pl.when((group > 0) | jnp.logical_not(aided & to_end(offset)))
            def _():
                for which in (K, V, Q):
                    seq_copy(which, group, offset).wait_send()

            seq_copy(CQ, group, offset).wait_send()

    loop(groups, sent_group)
    sent_aid()

    def sent_text(index):
        for hop in range(hops):
            for way in range(2):

                @pl.when(text_start_here(way, hop))
                def _():
                    text_copy(way, hop, index).wait_send()

    loop(chunks, sent_text)
    for which in range(2):
        for offset in range(1, chips):
            chip_copy(which, offset).wait_send()
        for offset in range(chips):
            pair_copy(which, offset).wait_send()
    own.wait()

    def out_group(group):
        for offset in offsets:
            out_copy(offset, group).wait()

    loop(groups, out_group)


def body(
    seq_size,
    prompt_size,
    queries,
    self_keys,
    self_values,
    cross_queries,
    context,
    key_weight,
    value_weight,
    lengths,
):
    tokens = queries.shape[1]
    full = tokens * seq_size
    width = key_weight.shape[1]
    model = context.shape[2]
    chips = prompt_size // CORES
    text_full = context.shape[1] * seq_size
    groups = width // HD // group_heads(width // HD)
    chunks = context.shape[1] // text_chunk(context.shape[1])
    activations = pltpu.VMEM((full, width), jnp.bfloat16)
    texts = pltpu.VMEM((text_full, width), jnp.bfloat16)
    dma = pltpu.SemaphoreType.DMA
    attended = pl.pallas_call(
        functools.partial(kernel, seq_size, prompt_size),
        out_shape=jax.ShapeDtypeStruct(queries.shape[1:], jnp.bfloat16),
        in_specs=[pl.BlockSpec(memory_space=pltpu.SMEM)]
        + [pl.BlockSpec(memory_space=pltpu.HBM)] * 7,
        out_specs=pl.BlockSpec(memory_space=pl.ANY),
        scratch_shapes=[activations] * 4
        + [pltpu.VMEM((text_full, model), jnp.bfloat16)]
        + [pltpu.VMEM((model, width), jnp.bfloat16)] * 2
        + [texts] * 2
        + [activations] * 2
        + [pltpu.VMEM((full, group_heads(width // HD) * HD), jnp.bfloat16)] * 4
        + [
            dma((8,)),
            dma((4, groups, seq_size)),
            dma((4, groups, seq_size)),
            dma((2, seq_size, chunks)),
            dma((2, seq_size, chunks)),
            dma((2, chips)),
            dma((2, chips)),
            dma((2, chips)),
            dma((2, chips)),
            dma((groups, seq_size)),
            dma((groups, seq_size)),
            pltpu.SemaphoreType.REGULAR((seq_size.bit_length(), 2)),
            pltpu.SemaphoreType.REGULAR((chips.bit_length(), chips.bit_length())),
            dma((3, 2)),
            dma((3, seq_size)),
            dma((3,)),
            dma((2,)),
        ],
        compiler_params=pltpu.CompilerParams(
            collective_id=0, has_side_effects=True, vmem_limit_bytes=48 * 1024 * 1024
        ),
    )(
        lengths,
        *(
            pltpu.with_memory_space_constraint(operand, pltpu.HBM)
            for operand in (
                queries[0],
                self_keys[0],
                self_values[0],
                cross_queries[0],
                context[0],
                key_weight,
                value_weight,
            )
        ),
    )
    return attended[None]


def solution(mesh):
    in_specs = (
        P("prompt", "seq", None),
        P("prompt", "seq", None),
        P("prompt", "seq", None),
        P("prompt", "seq", None),
        P("prompt", "seq", None),
        P("prompt", "seq"),
        P("prompt", "seq"),
        P("prompt"),
    )
    out_specs = P("prompt", "seq", None)
    step = functools.partial(body, mesh.shape["seq"], mesh.shape["prompt"])
    return jax.shard_map(step, mesh=mesh, in_specs=in_specs, out_specs=out_specs, check_vma=False)
```
